32 devices in a mesh: col: 8 (over z, y), row: 4 (over x, core).
Axes of the slice: x: 2, y: 2, z: 4, core: 2. Of those that a mesh axis runs over, the one named last changes fastest.
Arguments:
- sigma_anc: float32 [16, 16, 128, 128], P('row', 'col'), as said below
- panel_u: float32 [8, 8, 128, 128], P('col'), may hold values from -0.1875 to 0.1875
- structure: int32 [8, 8], P('col'), may hold values from 0 to 15, as said below
- diag_inv: float32 [8, 128, 128], P('col'), may hold values from -0.5 to 0.5
Outputs:
- panel_out: float32 [8, 16, 128, 128], P('col', 'row')
- diag_out: float32 [8, 128, 128], P('col')
The draws below stay inside these ranges and needn't reach their ends.
Inputs may be any that keep to these rules, and one draw needn't show every extreme that they name: `structure`: each row holds 8 different ancestor numbers in increasing order. `sigma_anc`: the matrix is symmetric: block (a, b) is the transpose of block (b, a).
All inputs are finite; a program needn't handle non-finite values.
Results may differ from the reference program's by a relative error of at most 0.0003.
Values sent between devices are 32-bit elements; how exact they have to be, the bound alone decides.
A program may use at most 128 MiB of HBM per device.

```python
import jax
import jax.numpy as jnp
from jax import lax

B = 128
NA = 16
K = 8
NS = 8


def draw_sigma_anc(key, part):
    side = NA * B
    base = jax.random.normal(jax.random.fold_in(key, 11), (side, side), jnp.float32)
    full = (base + base.T) * 0.7
    return full.reshape(NA, B, NA, B).transpose(0, 2, 1, 3)


def draw_structure(key, part):
    keys = jax.random.split(jax.random.fold_in(key, 17), NS)
    perms = jax.vmap(lambda k: jax.random.permutation(k, NA))(keys).astype(jnp.int32)
    chosen = perms[:, :K]
    inner = 1 + jax.random.permutation(jax.random.fold_in(key, 19), NA - 2)[:K - 2].astype(jnp.int32)
    first = jnp.concatenate([jnp.array([0, NA - 1], jnp.int32), inner])
    chosen = chosen.at[0].set(first)
    return jnp.sort(chosen, axis=1).astype(jnp.int32)


def block_levels(rng, dims, shards, low, high):
    gain, own = 1.0, jax.random.fold_in(rng, 6)
    for axis_at, blocks in shards:
        steps = jnp.exp(jax.random.uniform(jax.random.fold_in(own, axis_at), (blocks,), jnp.float32, low / len(shards), high / len(shards)))
        gain = gain * jnp.repeat(steps, dims[axis_at] // blocks).reshape([-1 if axis == axis_at else 1 for axis in range(len(dims))])
    return gain


def centred(key, shape, width, most, cuts=(), kind=jnp.bfloat16):
    level = block_levels(key, shape, cuts, -0.22, 0.18) if cuts else 1.0
    drawn = jax.random.normal(key, shape, jnp.float32) * width * level
    return jnp.minimum(jnp.maximum(drawn, -most), most).astype(kind)


def setup_inputs(seed: int = 0) -> dict:
    key_of = jax.random.split(jax.random.key(seed), 5)
    sigma_anc = draw_sigma_anc(jax.random.fold_in(key_of[4], 71), 0)
    panel_u = centred(key_of[1], (NS, K, B, B), (K * B) ** -0.5, 0.1875, ((0, 8),), jnp.float32)
    structure = draw_structure(jax.random.fold_in(key_of[4], 71), 0)
    diag_inv = centred(key_of[3], (NS, B, B), B ** -0.5, 0.5, ((0, 8),), jnp.float32)
    return dict(sigma_anc=sigma_anc, panel_u=panel_u, structure=structure, diag_inv=diag_inv)


def reference(sigma_anc, panel_u, structure, diag_inv):
    whole = sigma_anc.transpose(0, 2, 1, 3).reshape(NA * B, NA * B)
    offsets = jnp.arange(B, dtype=jnp.int32)
    ancestors = jnp.arange(NA, dtype=jnp.int32)

    def one_node(items):
        blocks, picks, inverse = items
        columns = (picks[:, None] * B + offsets[None, :]).reshape(-1).astype(jnp.int32)
        chosen = jnp.take(whole, columns, axis=1)
        stacked = blocks.reshape(K * B, B)
        result = jnp.dot(chosen, stacked, precision=lax.Precision.HIGHEST, preferred_element_type=jnp.float32)
        member = jnp.any(picks[None, :] == ancestors[:, None], axis=1).astype(jnp.float32)
        panel = -result.reshape(NA, B, B) * member[:, None, None]
        onehot = (picks[:, None] == ancestors[None, :]).astype(jnp.float32)
        dense = jnp.einsum("ka,kxy->axy", onehot, blocks, precision=lax.Precision.HIGHEST)
        update = jnp.dot(dense.reshape(NA * B, B).T, panel.reshape(NA * B, B), precision=lax.Precision.HIGHEST, preferred_element_type=jnp.float32)
        base = jnp.dot(inverse.T, inverse, precision=lax.Precision.HIGHEST, preferred_element_type=jnp.float32)
        return panel, base - update

    panel_out, diag_out = lax.map(one_node, (panel_u, structure, diag_inv))
    return panel_out, diag_out
```

```python
import functools

import jax
import jax.numpy as jnp
from jax import lax
from jax.experimental import pallas as pl
from jax.experimental.pallas import tpu as pltpu
from jax.sharding import PartitionSpec as P

MESH = pl.DeviceIdType.MESH
HIGHEST = lax.Precision.HIGHEST


def split(x):
    high = x.astype(jnp.bfloat16)
    return high, (x - high.astype(jnp.float32)).astype(jnp.bfloat16)


def dot_t(a, b):
    return lax.dot_general(
        a, b, (((0,), (0,)), ((), ())), precision=HIGHEST, preferred_element_type=jnp.float32
    )


def kernel(
    planes,
    rows,
    chunks,
    sigma_ref,
    u_ref,
    s_ref,
    inv_ref,
    panel_ref,
    diag_ref,
    dense,
    moved,
    other,
    sig_hi,
    sig_lo,
    w_cat,
    sums,
    came,
    share,
    shares,
    y_send,
    y_recv,
    w_send,
    w_recv,
    f_send,
    f_recv,
    r_send,
    r_recv,
    d_send,
    d_recv,
):
    row_count, col_count, width = sigma_ref.shape[0], sigma_ref.shape[1], sigma_ref.shape[2]
    plane_cols = 2 * col_count
    step_rows = row_count // chunks
    col, row = lax.axis_index("col"), lax.axis_index("row")
    z, y = col // 2, col % 2
    half = row % 2
    mate = row + 1 - 2 * half
    entries = u_ref.shape[1]

    def at(plane, lane=None, line=None):
        lane = y if lane is None else lane
        return {"col": plane * 2 + lane, "row": row if line is None else line}

    def order(n):
        right_first = jnp.where(n < planes - 1 - z, planes - 1 - n, n - (planes - 1 - z))
        left_first = jnp.where(n < z, n, planes - 1 - (n - z))
        return jnp.where(2 * z < planes, right_first, left_first)

    barrier = pltpu.get_barrier_semaphore()
    pl.semaphore_signal(barrier, inc=1, device_id=at(z, 1 - y), device_id_type=MESH)

    @pl.loop(0, planes - 1)
    def _(n):
        pl.semaphore_signal(barrier, inc=1, device_id=at(order(n)), device_id_type=MESH)

    for o in range(1, rows):
        pl.semaphore_signal(
            barrier, inc=1, device_id=at(z, None, lax.rem(row + o, rows)), device_id_type=MESH
        )

    def member(b):
        found, where = jnp.int32(0), jnp.int32(0)
        for k in range(entries):
            hit = s_ref[0, k] == b
            found, where = jnp.where(hit, 1, found), jnp.where(hit, k, where)
        return found.astype(jnp.float32), where

    @pl.loop(0, dense.shape[0])
    def _(b):
        found, where = member(b)
        dense[b] = u_ref[0, where] * found

    inv = inv_ref[0]
    diag_ref[0] = dot_t(inv, inv)

    def plane_part(plane, part):
        lane = jnp.where(part == 0, y, 1 - y)
        return plane * plane_cols + lane * col_count

    for part in range(2):
        for i in range(col_count):
            moved[z, part * col_count + i] = dense[plane_part(z, part) + i]

    pl.semaphore_wait(barrier, planes - 1 + 1 + rows - 1)

    def y_copy(c):
        rng = pl.ds(c * step_rows, step_rows)
        return pltpu.make_async_remote_copy(
            sigma_ref.at[rng], other.at[rng], y_send.at[c], y_recv.at[c], at(z, 1 - y), MESH
        )

    def w_copy(target):
        return pltpu.make_async_remote_copy(
            dense.at[pl.ds(plane_part(target, half), col_count)],
            moved.at[z, pl.ds(half * col_count, col_count)],
            w_send.at[target],
            w_recv.at[z],
            at(target),
            MESH,
        )

    def w_arrival(source):
        mine = moved.at[source, pl.ds(half * col_count, col_count)]
        return pltpu.make_async_remote_copy(
            mine, mine, w_send.at[source], w_recv.at[source], at(source), MESH
        )

    def f_copy(source):
        mine = moved.at[source, pl.ds(half * col_count, col_count)]
        return pltpu.make_async_remote_copy(
            mine, mine, f_send.at[source], f_recv.at[source], at(z, None, mate), MESH
        )

    def f_arrival(source):
        theirs = moved.at[source, pl.ds((1 - half) * col_count, col_count)]
        return pltpu.make_async_remote_copy(
            theirs, theirs, f_send.at[source], f_recv.at[source], at(z, None, mate), MESH
        )

    def r_copy(d, c, slot, target):
        rng = pl.ds(c * step_rows, step_rows)
        return pltpu.make_async_remote_copy(
            sums.at[d, rng], came.at[slot, rng], r_send.at[d, c], r_recv.at[slot, c], at(target), MESH
        )

    def r_arrival(slot, c):
        rng = pl.ds(c * step_rows, step_rows)
        return pltpu.make_async_remote_copy(
            came.at[slot, rng], came.at[slot, rng], r_send.at[0, c], r_recv.at[slot, c], at(z, 1 - y), MESH
        )

    for c in range(chunks):
        y_copy(c).start()

    @pl.loop(0, planes - 1)
    def _(n):
        w_copy(order(n)).start()

    def forward(source):
        w_arrival(source).wait_recv()
        f_copy(source).start()

    def load_w(d):
        for i in range(plane_cols):
            high, low = split(moved[d, i])
            w_cat[i * width : (i + 1) * width, :width] = high
            w_cat[i * width : (i + 1) * width, width:] = low

    def convert(c):
        for q in range(step_rows):
            a = c * step_rows + q
            for source, base in ((sigma_ref, 0), (other, col_count)):
                for i in range(col_count):
                    high, low = split(source[a, i])
                    lanes = slice((base + i) * width, (base + i + 1) * width)
                    sig_hi[a, :, lanes] = high
                    sig_lo[a, :, lanes] = low

    def product(a):
        both = jnp.dot(sig_hi[a], w_cat[...], preferred_element_type=jnp.float32)
        low = jnp.dot(sig_lo[a], w_cat[:, :width], preferred_element_type=jnp.float32)
        return both[:, :width] + (both[:, width:] + low)

    forward(order(0))

    @pl.loop(0, planes - 1)
    def _(n):
        d = order(n)
        right = d > z
        f_arrival(d).wait_recv()
        load_w(d)
        has_up = jnp.where(right, z > 0, z < planes - 1)
        target = jnp.where(right, z + 1, z - 1)
        slot = jnp.where(right, d, jnp.where(d == z - 1, planes, d))
        for c in range(chunks):

            @pl.when(n == 0)
            def _():
                y_copy(c).wait_recv()
                convert(c)

            for q in range(step_rows):
                a = c * step_rows + q
                sums[d, a] = product(a)

            @pl.when(has_up)
            def _():
                r_arrival(d, c).wait_recv()
                for q in range(step_rows):
                    a = c * step_rows + q
                    sums[d, a] += came[d, a]

            r_copy(d, c, slot, target).start()

            if c == chunks // 2:

                @pl.when(n + 1 < planes - 1)
                def _():
                    forward(order(n + 1))

    load_w(z)
    for a in range(row_count):
        sums[z, a] = product(a)
    row_start = row * row_count
    total = jnp.zeros((width, width), jnp.float32)
    for c in range(chunks):

        @pl.when(z > 0)
        def _():
            r_arrival(z, c).wait_recv()
            for q in range(step_rows):
                a = c * step_rows + q
                sums[z, a] += came[z, a]

        @pl.when(z < planes - 1)
        def _():
            r_arrival(planes, c).wait_recv()
            for q in range(step_rows):
                a = c * step_rows + q
                sums[z, a] += came[planes, a]

        for q in range(step_rows):
            a = c * step_rows + q
            found, _ = member(row_start + a)
            panel = -sums[z, a] * found
            panel_ref[0, a] = panel
            total += dot_t(dense[row_start + a], panel)
    share[...] = total

    def d_copy(o):
        return pltpu.make_async_remote_copy(
            share,
            shares.at[o - 1],
            d_send.at[o - 1],
            d_recv.at[o - 1],
            at(z, None, lax.rem(row + o, rows)),
            MESH,
        )

    for o in range(1, rows):
        d_copy(o).start()
    diag_ref[0] -= total
    for o in range(1, rows):
        d_copy(o).wait_recv()
        diag_ref[0] -= shares[o - 1]

    for o in range(1, rows):
        d_copy(o).wait_send()
    for c in range(chunks):
        y_copy(c).wait_send()

    @pl.loop(0, planes - 1)
    def _(n):
        d = order(n)
        w_copy(d).wait_send()
        f_copy(d).wait_send()
        for c in range(chunks):
            r_copy(d, c, d, d).wait_send()


def local(sigma_anc, panel_u, structure, diag_inv):
    row_count, col_count, width = sigma_anc.shape[0], sigma_anc.shape[1], sigma_anc.shape[2]
    cols, rows = lax.axis_size("col"), lax.axis_size("row")
    planes = cols // 2
    plane_cols = 2 * col_count
    chunks = next(c for c in (4, 2, 1) if row_count % c == 0)
    block = (width, width)
    f32, bf16 = jnp.float32, jnp.bfloat16
    vmem = pl.BlockSpec(memory_space=pltpu.VMEM)
    dma = pltpu.SemaphoreType.DMA
    return pl.pallas_call(
        functools.partial(kernel, planes, rows, chunks),
        out_shape=(
            jax.ShapeDtypeStruct((1, row_count, *block), f32),
            jax.ShapeDtypeStruct((1, *block), f32),
        ),
        in_specs=[vmem, vmem, pl.BlockSpec(memory_space=pltpu.SMEM), vmem],
        out_specs=(vmem, vmem),
        scratch_shapes=[
            pltpu.VMEM((cols * col_count, *block), f32),
            pltpu.VMEM((planes, plane_cols, *block), f32),
            pltpu.VMEM((row_count, col_count, *block), f32),
            pltpu.VMEM((row_count, width, plane_cols * width), bf16),
            pltpu.VMEM((row_count, width, plane_cols * width), bf16),
            pltpu.VMEM((plane_cols * width, 2 * width), bf16),
            pltpu.VMEM((planes, row_count, *block), f32),
            pltpu.VMEM((planes + 1, row_count, *block), f32),
            pltpu.VMEM(block, f32),
            pltpu.VMEM((rows - 1, *block), f32),
            dma((chunks,)),
            dma((chunks,)),
            dma((planes,)),
            dma((planes,)),
            dma((planes,)),
            dma((planes,)),
            dma((planes, chunks)),
            dma((planes + 1, chunks)),
            dma((rows - 1,)),
            dma((rows - 1,)),
        ],
        compiler_params=pltpu.CompilerParams(
            collective_id=0, has_side_effects=True, vmem_limit_bytes=60 * 1024 * 1024
        ),
    )(sigma_anc, panel_u, structure, diag_inv)


def solution(mesh):
    placed = (
        P("row", "col", None, None),
        P("col", None, None, None),
        P("col", None),
        P("col", None, None),
    )
    return jax.shard_map(
        local,
        mesh=mesh,
        in_specs=placed,
        out_specs=(P("col", "row", None, None), P("col", None, None)),
        check_vma=False,
    )
```

```python
import functools

import jax
import jax.numpy as jnp
from jax import lax
from jax.experimental import pallas as pl
from jax.experimental.pallas import tpu as pltpu
from jax.sharding import PartitionSpec as P

MESH = pl.DeviceIdType.MESH
HIGHEST = lax.Precision.HIGHEST


def split(x):
    high = x.astype(jnp.bfloat16)
    return high, (x - high.astype(jnp.float32)).astype(jnp.bfloat16)


def dot_t(a, b):
    return lax.dot_general(
        a, b, (((0,), (0,)), ((), ())), precision=HIGHEST, preferred_element_type=jnp.float32
    )


def kernel(
    planes,
    rows,
    chunks,
    sigma_ref,
    u_ref,
    s_ref,
    inv_ref,
    panel_ref,
    diag_ref,
    held,
    u_held,
    dense,
    moved,
    other,
    sig_hi,
    sig_lo,
    w_cat,
    sums,
    came,
    share,
    shares,
    y_send,
    y_recv,
    w_send,
    w_recv,
    f_send,
    f_recv,
    r_send,
    r_recv,
    d_send,
    d_recv,
    in_sem,
):
    row_count, col_count, width = sigma_ref.shape[0], sigma_ref.shape[1], sigma_ref.shape[2]
    plane_cols = 2 * col_count
    step_rows = row_count // chunks
    col, row = lax.axis_index("col"), lax.axis_index("row")
    z, y = col // 2, col % 2
    half = row % 2
    mate = row + 1 - 2 * half
    entries = u_ref.shape[1]

    def at(plane, lane=None, line=None):
        lane = y if lane is None else lane
        return {"col": plane * 2 + lane, "row": row if line is None else line}

    def order(n):
        right_first = jnp.where(n < planes - 1 - z, planes - 1 - n, n - (planes - 1 - z))
        left_first = jnp.where(n < z, n, planes - 1 - (n - z))
        return jnp.where(2 * z < planes, right_first, left_first)

    u_in = pltpu.make_async_copy(u_ref, u_held, in_sem.at[0])
    sigma_in = pltpu.make_async_copy(sigma_ref, held, in_sem.at[1])
    u_in.start()
    sigma_in.start()

    barrier = pltpu.get_barrier_semaphore()
    pl.semaphore_signal(barrier, inc=1, device_id=at(z, 1 - y), device_id_type=MESH)

    @pl.loop(0, planes - 1)
    def _(n):
        pl.semaphore_signal(barrier, inc=1, device_id=at(order(n)), device_id_type=MESH)

    for o in range(1, rows):
        pl.semaphore_signal(
            barrier, inc=1, device_id=at(z, None, lax.rem(row + o, rows)), device_id_type=MESH
        )

    def member(b):
        found, where = jnp.int32(0), jnp.int32(0)
        for k in range(entries):
            hit = s_ref[0, k] == b
            found, where = jnp.where(hit, 1, found), jnp.where(hit, k, where)
        return found.astype(jnp.float32), where

    u_in.wait()

    @pl.loop(0, dense.shape[0])
    def _(b):
        found, where = member(b)
        dense[b] = u_held[0, where] * found

    def plane_part(plane, part):
        lane = jnp.where(part == 0, y, 1 - y)
        return plane * plane_cols + lane * col_count

    for part in range(2):
        for i in range(col_count):
            moved[z, part * col_count + i] = dense[plane_part(z, part) + i]

    pl.semaphore_wait(barrier, planes - 1 + 1 + rows - 1)

    def y_copy(c):
        rng = pl.ds(c * step_rows, step_rows)
        return pltpu.make_async_remote_copy(
            sigma_ref.at[rng], other.at[rng], y_send.at[c], y_recv.at[c], at(z, 1 - y), MESH
        )

    def w_copy(target):
        return pltpu.make_async_remote_copy(
            dense.at[pl.ds(plane_part(target, half), col_count)],
            moved.at[z, pl.ds(half * col_count, col_count)],
            w_send.at[target],
            w_recv.at[z],
            at(target),
            MESH,
        )

    def w_arrival(source):
        mine = moved.at[source, pl.ds(half * col_count, col_count)]
        return pltpu.make_async_remote_copy(
            mine, mine, w_send.at[source], w_recv.at[source], at(source), MESH
        )

    def f_copy(source):
        mine = moved.at[source, pl.ds(half * col_count, col_count)]
        return pltpu.make_async_remote_copy(
            mine, mine, f_send.at[source], f_recv.at[source], at(z, None, mate), MESH
        )

    def f_arrival(source):
        theirs = moved.at[source, pl.ds((1 - half) * col_count, col_count)]
        return pltpu.make_async_remote_copy(
            theirs, theirs, f_send.at[source], f_recv.at[source], at(z, None, mate), MESH
        )

    def r_copy(d, c, slot, target):
        rng = pl.ds(c * step_rows, step_rows)
        return pltpu.make_async_remote_copy(
            sums.at[d, rng], came.at[slot, rng], r_send.at[d, c], r_recv.at[slot, c], at(target), MESH
        )

    def r_arrival(slot, c):
        rng = pl.ds(c * step_rows, step_rows)
        return pltpu.make_async_remote_copy(
            came.at[slot, rng], came.at[slot, rng], r_send.at[0, c], r_recv.at[slot, c], at(z, 1 - y), MESH
        )

    for c in range(chunks):
        y_copy(c).start()

    @pl.loop(0, planes - 1)
    def _(n):
        w_copy(order(n)).start()

    def forward(source):
        w_arrival(source).wait_recv()
        f_copy(source).start()

    def load_w(d):
        for i in range(plane_cols):
            high, low = split(moved[d, i])
            w_cat[d, i * width : (i + 1) * width, :width] = high
            w_cat[d, i * width : (i + 1) * width, width:] = low

    def convert(c):
        for q in range(step_rows):
            a = c * step_rows + q
            for source, base in ((held, 0), (other, col_count)):
                for i in range(col_count):
                    high, low = split(source[a, i])
                    lanes = slice((base + i) * width, (base + i + 1) * width)
                    sig_hi[a, :, lanes] = high
                    sig_lo[a, :, lanes] = low

    def product(a, d):
        both = jnp.dot(sig_hi[a], w_cat[d], preferred_element_type=jnp.float32)
        low = jnp.dot(sig_lo[a], w_cat[d, :, :width], preferred_element_type=jnp.float32)
        return both[:, :width] + (both[:, width:] + low)

    row_start = row * row_count

    def own(c):
        for q in range(step_rows):
            sums[z, c * step_rows + q] = product(c * step_rows + q, z)

        @pl.when(z > 0)
        def _():
            r_arrival(z, c).wait_recv()
            for q in range(step_rows):
                a = c * step_rows + q
                sums[z, a] += came[z, a]

        @pl.when(z < planes - 1)
        def _():
            r_arrival(planes, c).wait_recv()
            for q in range(step_rows):
                a = c * step_rows + q
                sums[z, a] += came[planes, a]

        for q in range(step_rows):
            a = c * step_rows + q
            found, _ = member(row_start + a)
            panel = -sums[z, a] * found
            panel_ref[0, a] = panel
            share[...] += dot_t(dense[row_start + a], panel)

    inv = inv_ref[0]
    diag_ref[0] = dot_t(inv, inv)
    share[...] = jnp.zeros_like(share)
    load_w(z)
    sigma_in.wait()
    forward(order(0))
    y_copy(0).wait_recv()
    convert(0)

    @pl.loop(0, chunks)
    def _(c):
        @pl.loop(0, planes - 1)
        def _(n):
            d = order(n)
            right = d > z
            has_up = jnp.where(right, z > 0, z < planes - 1)
            target = jnp.where(right, z + 1, z - 1)
            slot = jnp.where(right, d, jnp.where(d == z - 1, planes, d))

            @pl.when(c == 0)
            def _():
                @pl.when(n + 1 < planes - 1)
                def _():
                    forward(order(n + 1))

                f_arrival(d).wait_recv()
                load_w(d)

            for q in range(step_rows):
                a = c * step_rows + q
                sums[d, a] = product(a, d)

            @pl.when(has_up)
            def _():
                r_arrival(d, c).wait_recv()
                for q in range(step_rows):
                    a = c * step_rows + q
                    sums[d, a] += came[d, a]

            r_copy(d, c, slot, target).start()

        @pl.when(c + 1 < chunks)
        def _():
            y_copy(c + 1).wait_recv()
            convert(c + 1)

        @pl.when(c > 0)
        def _():
            own(c - 1)

    own(chunks - 1)
    total = share[...]

    def d_copy(o):
        return pltpu.make_async_remote_copy(
            share,
            shares.at[o - 1],
            d_send.at[o - 1],
            d_recv.at[o - 1],
            at(z, None, lax.rem(row + o, rows)),
            MESH,
        )

    for o in range(1, rows):
        d_copy(o).start()
    diag_ref[0] -= total
    for o in range(1, rows):
        d_copy(o).wait_recv()
        diag_ref[0] -= shares[o - 1]

    for o in range(1, rows):
        d_copy(o).wait_send()
    for c in range(chunks):
        y_copy(c).wait_send()

    @pl.loop(0, planes - 1)
    def _(n):
        d = order(n)
        w_copy(d).wait_send()
        f_copy(d).wait_send()
        for c in range(chunks):
            r_copy(d, c, d, d).wait_send()


def local(sigma_anc, panel_u, structure, diag_inv):
    row_count, col_count, width = sigma_anc.shape[0], sigma_anc.shape[1], sigma_anc.shape[2]
    cols, rows = lax.axis_size("col"), lax.axis_size("row")
    planes = cols // 2
    plane_cols = 2 * col_count
    chunks = next(c for c in (4, 2, 1) if row_count % c == 0)
    block = (width, width)
    f32, bf16 = jnp.float32, jnp.bfloat16
    vmem = pl.BlockSpec(memory_space=pltpu.VMEM)
    hbm = pl.BlockSpec(memory_space=pl.ANY)
    dma = pltpu.SemaphoreType.DMA
    return pl.pallas_call(
        functools.partial(kernel, planes, rows, chunks),
        out_shape=(
            jax.ShapeDtypeStruct((1, row_count, *block), f32),
            jax.ShapeDtypeStruct((1, *block), f32),
        ),
        in_specs=[hbm, hbm, pl.BlockSpec(memory_space=pltpu.SMEM), vmem],
        out_specs=(vmem, vmem),
        scratch_shapes=[
            pltpu.VMEM(sigma_anc.shape, f32),
            pltpu.VMEM(panel_u.shape, f32),
            pltpu.VMEM((cols * col_count, *block), f32),
            pltpu.VMEM((planes, plane_cols, *block), f32),
            pltpu.VMEM((row_count, col_count, *block), f32),
            pltpu.VMEM((row_count, width, plane_cols * width), bf16),
            pltpu.VMEM((row_count, width, plane_cols * width), bf16),
            pltpu.VMEM((planes, plane_cols * width, 2 * width), bf16),
            pltpu.VMEM((planes, row_count, *block), f32),
            pltpu.VMEM((planes + 1, row_count, *block), f32),
            pltpu.VMEM(block, f32),
            pltpu.VMEM((rows - 1, *block), f32),
            dma((chunks,)),
            dma((chunks,)),
            dma((planes,)),
            dma((planes,)),
            dma((planes,)),
            dma((planes,)),
            dma((planes, chunks)),
            dma((planes + 1, chunks)),
            dma((rows - 1,)),
            dma((rows - 1,)),
            dma((2,)),
        ],
        compiler_params=pltpu.CompilerParams(
            collective_id=0, has_side_effects=True, vmem_limit_bytes=60 * 1024 * 1024
        ),
    )(sigma_anc, panel_u, structure, diag_inv)


def solution(mesh):
    placed = (
        P("row", "col", None, None),
        P("col", None, None, None),
        P("col", None),
        P("col", None, None),
    )
    return jax.shard_map(
        local,
        mesh=mesh,
        in_specs=placed,
        out_specs=(P("col", "row", None, None), P("col", None, None)),
        check_vma=False,
    )
```

```python
import functools

import jax
import jax.numpy as jnp
from jax import lax
from jax.experimental import pallas as pl
from jax.experimental.pallas import tpu as pltpu
from jax.sharding import PartitionSpec as P

MESH = pl.DeviceIdType.MESH
HIGHEST = lax.Precision.HIGHEST


def split(x):
    high = x.astype(jnp.bfloat16)
    return high, (x - high.astype(jnp.float32)).astype(jnp.bfloat16)


def dot_t(a, b):
    return lax.dot_general(
        a, b, (((0,), (0,)), ((), ())), precision=HIGHEST, preferred_element_type=jnp.float32
    )


def kernel(
    planes,
    rows,
    chunks,
    sigma_ref,
    u_ref,
    s_ref,
    inv_ref,
    panel_ref,
    diag_ref,
    dense,
    moved,
    other,
    sig_hi,
    sig_lo,
    w_cat,
    sums,
    came,
    share,
    shares,
    y_send,
    y_recv,
    w_send,
    w_recv,
    f_send,
    f_recv,
    r_send,
    r_recv,
    d_send,
    d_recv,
):
    row_count, col_count, width = sigma_ref.shape[0], sigma_ref.shape[1], sigma_ref.shape[2]
    plane_cols = 2 * col_count
    step_rows = row_count // chunks
    col, row = lax.axis_index("col"), lax.axis_index("row")
    z, y = col // 2, col % 2
    half = row % 2
    mate = row + 1 - 2 * half
    entries = u_ref.shape[1]

    def at(plane, lane=None, line=None):
        lane = y if lane is None else lane
        return {"col": plane * 2 + lane, "row": row if line is None else line}

    def order(n):
        right_first = jnp.where(n < planes - 1 - z, planes - 1 - n, n - (planes - 1 - z))
        left_first = jnp.where(n < z, n, planes - 1 - (n - z))
        return jnp.where(2 * z < planes, right_first, left_first)

    barrier = pltpu.get_barrier_semaphore()
    pl.semaphore_signal(barrier, inc=1, device_id=at(z, 1 - y), device_id_type=MESH)

    @pl.loop(0, planes - 1)
    def _(n):
        pl.semaphore_signal(barrier, inc=1, device_id=at(order(n)), device_id_type=MESH)

    for o in range(1, rows):
        pl.semaphore_signal(
            barrier, inc=1, device_id=at(z, None, lax.rem(row + o, rows)), device_id_type=MESH
        )

    def member(b):
        found, where = jnp.int32(0), jnp.int32(0)
        for k in range(entries):
            hit = s_ref[0, k] == b
            found, where = jnp.where(hit, 1, found), jnp.where(hit, k, where)
        return found.astype(jnp.float32), where

    @pl.loop(0, dense.shape[0])
    def _(b):
        found, where = member(b)
        dense[b] = u_ref[0, where] * found

    inv = inv_ref[0]
    diag_ref[0] = dot_t(inv, inv)

    def plane_part(plane, part):
        lane = jnp.where(part == 0, y, 1 - y)
        return plane * plane_cols + lane * col_count

    for part in range(2):
        for i in range(col_count):
            moved[z, part * col_count + i] = dense[plane_part(z, part) + i]

    pl.semaphore_wait(barrier, planes - 1 + 1 + rows - 1)

    def y_copy(c):
        rng = pl.ds(c * step_rows, step_rows)
        return pltpu.make_async_remote_copy(
            sigma_ref.at[rng], other.at[rng], y_send.at[c], y_recv.at[c], at(z, 1 - y), MESH
        )

    def w_copy(target):
        return pltpu.make_async_remote_copy(
            dense.at[pl.ds(plane_part(target, half), col_count)],
            moved.at[z, pl.ds(half * col_count, col_count)],
            w_send.at[target],
            w_recv.at[z],
            at(target),
            MESH,
        )

    def w_arrival(source):
        mine = moved.at[source, pl.ds(half * col_count, col_count)]
        return pltpu.make_async_remote_copy(
            mine, mine, w_send.at[source], w_recv.at[source], at(source), MESH
        )

    def f_copy(source):
        mine = moved.at[source, pl.ds(half * col_count, col_count)]
        return pltpu.make_async_remote_copy(
            mine, mine, f_send.at[source], f_recv.at[source], at(z, None, mate), MESH
        )

    def f_arrival(source):
        theirs = moved.at[source, pl.ds((1 - half) * col_count, col_count)]
        return pltpu.make_async_remote_copy(
            theirs, theirs, f_send.at[source], f_recv.at[source], at(z, None, mate), MESH
        )

    def r_copy(d, c, slot, target):
        rng = pl.ds(c * step_rows, step_rows)
        return pltpu.make_async_remote_copy(
            sums.at[d, rng], came.at[slot, rng], r_send.at[d, c], r_recv.at[slot, c], at(target), MESH
        )

    def r_arrival(slot, c):
        rng = pl.ds(c * step_rows, step_rows)
        return pltpu.make_async_remote_copy(
            came.at[slot, rng], came.at[slot, rng], r_send.at[0, c], r_recv.at[slot, c], at(z, 1 - y), MESH
        )

    for c in range(chunks):
        y_copy(c).start()

    @pl.loop(0, planes - 1)
    def _(n):
        w_copy(order(n)).start()

    def forward(source):
        w_arrival(source).wait_recv()
        f_copy(source).start()

    def load_w(d):
        for i in range(plane_cols):
            high, low = split(moved[d, i])
            w_cat[i * width : (i + 1) * width, :width] = high
            w_cat[i * width : (i + 1) * width, width:] = low

    def convert(c):
        for q in range(step_rows):
            a = c * step_rows + q
            for source, base in ((sigma_ref, 0), (other, col_count)):
                for i in range(col_count):
                    high, low = split(source[a, i])
                    lanes = slice((base + i) * width, (base + i + 1) * width)
                    sig_hi[a, :, lanes] = high
                    sig_lo[a, :, lanes] = low

    def product(a):
        both = jnp.dot(sig_hi[a], w_cat[...], preferred_element_type=jnp.float32)
        low = jnp.dot(sig_lo[a], w_cat[:, :width], preferred_element_type=jnp.float32)
        return both[:, :width] + (both[:, width:] + low)

    forward(order(0))

    @pl.loop(0, planes - 1)
    def _(n):
        d = order(n)
        right = d > z
        f_arrival(d).wait_recv()
        load_w(d)
        has_up = jnp.where(right, z > 0, z < planes - 1)
        target = jnp.where(right, z + 1, z - 1)
        slot = jnp.where(right, d, jnp.where(d == z - 1, planes, d))
        for c in range(chunks):

            @pl.when(n == 0)
            def _():
                y_copy(c).wait_recv()
                convert(c)

            for q in range(step_rows):
                a = c * step_rows + q
                sums[d, a] = product(a)

            @pl.when(has_up)
            def _():
                r_arrival(d, c).wait_recv()
                for q in range(step_rows):
                    a = c * step_rows + q
                    sums[d, a] += came[d, a]

            r_copy(d, c, slot, target).start()

            if c == 0:

                @pl.when(n + 1 < planes - 1)
                def _():
                    forward(order(n + 1))

    load_w(z)
    for a in range(row_count):
        sums[z, a] = product(a)
    row_start = row * row_count
    total = jnp.zeros((width, width), jnp.float32)
    for c in range(chunks):

        @pl.when(z > 0)
        def _():
            r_arrival(z, c).wait_recv()
            for q in range(step_rows):
                a = c * step_rows + q
                sums[z, a] += came[z, a]

        @pl.when(z < planes - 1)
        def _():
            r_arrival(planes, c).wait_recv()
            for q in range(step_rows):
                a = c * step_rows + q
                sums[z, a] += came[planes, a]

        for q in range(step_rows):
            a = c * step_rows + q
            found, _ = member(row_start + a)
            panel = -sums[z, a] * found
            panel_ref[0, a] = panel
            total += dot_t(dense[row_start + a], panel)
    share[...] = total

    def d_copy(o):
        return pltpu.make_async_remote_copy(
            share,
            shares.at[o - 1],
            d_send.at[o - 1],
            d_recv.at[o - 1],
            at(z, None, lax.rem(row + o, rows)),
            MESH,
        )

    for o in range(1, rows):
        d_copy(o).start()
    diag_ref[0] -= total
    for o in range(1, rows):
        d_copy(o).wait_recv()
        diag_ref[0] -= shares[o - 1]

    for o in range(1, rows):
        d_copy(o).wait_send()
    for c in range(chunks):
        y_copy(c).wait_send()

    @pl.loop(0, planes - 1)
    def _(n):
        d = order(n)
        w_copy(d).wait_send()
        f_copy(d).wait_send()
        for c in range(chunks):
            r_copy(d, c, d, d).wait_send()


def local(sigma_anc, panel_u, structure, diag_inv):
    row_count, col_count, width = sigma_anc.shape[0], sigma_anc.shape[1], sigma_anc.shape[2]
    cols, rows = lax.axis_size("col"), lax.axis_size("row")
    planes = cols // 2
    plane_cols = 2 * col_count
    chunks = next(c for c in (4, 2, 1) if row_count % c == 0)
    block = (width, width)
    f32, bf16 = jnp.float32, jnp.bfloat16
    vmem = pl.BlockSpec(memory_space=pltpu.VMEM)
    dma = pltpu.SemaphoreType.DMA
    return pl.pallas_call(
        functools.partial(kernel, planes, rows, chunks),
        out_shape=(
            jax.ShapeDtypeStruct((1, row_count, *block), f32),
            jax.ShapeDtypeStruct((1, *block), f32),
        ),
        in_specs=[vmem, vmem, pl.BlockSpec(memory_space=pltpu.SMEM), vmem],
        out_specs=(vmem, vmem),
        scratch_shapes=[
            pltpu.VMEM((cols * col_count, *block), f32),
            pltpu.VMEM((planes, plane_cols, *block), f32),
            pltpu.VMEM((row_count, col_count, *block), f32),
            pltpu.VMEM((row_count, width, plane_cols * width), bf16),
            pltpu.VMEM((row_count, width, plane_cols * width), bf16),
            pltpu.VMEM((plane_cols * width, 2 * width), bf16),
            pltpu.VMEM((planes, row_count, *block), f32),
            pltpu.VMEM((planes + 1, row_count, *block), f32),
            pltpu.VMEM(block, f32),
            pltpu.VMEM((rows - 1, *block), f32),
            dma((chunks,)),
            dma((chunks,)),
            dma((planes,)),
            dma((planes,)),
            dma((planes,)),
            dma((planes,)),
            dma((planes, chunks)),
            dma((planes + 1, chunks)),
            dma((rows - 1,)),
            dma((rows - 1,)),
        ],
        compiler_params=pltpu.CompilerParams(
            collective_id=0, has_side_effects=True, vmem_limit_bytes=60 * 1024 * 1024
        ),
    )(sigma_anc, panel_u, structure, diag_inv)


def solution(mesh):
    placed = (
        P("row", "col", None, None),
        P("col", None, None, None),
        P("col", None),
        P("col", None, None),
    )
    return jax.shard_map(
        local,
        mesh=mesh,
        in_specs=placed,
        out_specs=(P("col", "row", None, None), P("col", None, None)),
        check_vma=False,
    )
```

```python
import functools

import jax
import jax.numpy as jnp
from jax import lax
from jax.experimental import pallas as pl
from jax.experimental.pallas import tpu as pltpu
from jax.sharding import PartitionSpec as P

MESH = pl.DeviceIdType.MESH
HIGHEST = lax.Precision.HIGHEST


def split(x):
    high = x.astype(jnp.bfloat16)
    return high, (x - high.astype(jnp.float32)).astype(jnp.bfloat16)


def dot_t(a, b):
    return lax.dot_general(
        a, b, (((0,), (0,)), ((), ())), precision=HIGHEST, preferred_element_type=jnp.float32
    )


def kernel(
    planes,
    rows,
    chunks,
    sigma_ref,
    u_ref,
    s_ref,
    inv_ref,
    panel_ref,
    diag_ref,
    dense,
    moved,
    other,
    sig_hi,
    sig_lo,
    w_cat,
    sums,
    came,
    share,
    shares,
    y_send,
    y_recv,
    w_send,
    w_recv,
    f_send,
    f_recv,
    r_send,
    r_recv,
    d_send,
    d_recv,
):
    row_count, col_count, width = sigma_ref.shape[0], sigma_ref.shape[1], sigma_ref.shape[2]
    plane_cols = 2 * col_count
    step_rows = row_count // chunks
    col, row = lax.axis_index("col"), lax.axis_index("row")
    z, y = col // 2, col % 2
    half = row % 2
    mate = row + 1 - 2 * half
    entries = u_ref.shape[1]

    def at(plane, lane=None, line=None):
        lane = y if lane is None else lane
        return {"col": plane * 2 + lane, "row": row if line is None else line}

    def order(n):
        right_first = jnp.where(n < planes - 1 - z, planes - 1 - n, n - (planes - 1 - z))
        left_first = jnp.where(n < z, n, planes - 1 - (n - z))
        return jnp.where(2 * z < planes, right_first, left_first)

    barrier = pltpu.get_barrier_semaphore()
    pl.semaphore_signal(barrier, inc=1, device_id=at(z, 1 - y), device_id_type=MESH)

    @pl.loop(0, planes - 1)
    def _(n):
        pl.semaphore_signal(barrier, inc=1, device_id=at(order(n)), device_id_type=MESH)

    for o in range(1, rows):
        pl.semaphore_signal(
            barrier, inc=1, device_id=at(z, None, lax.rem(row + o, rows)), device_id_type=MESH
        )

    def member(b):
        found, where = jnp.int32(0), jnp.int32(0)
        for k in range(entries):
            hit = s_ref[0, k] == b
            found, where = jnp.where(hit, 1, found), jnp.where(hit, k, where)
        return found.astype(jnp.float32), where

    @pl.loop(0, dense.shape[0])
    def _(b):
        found, where = member(b)
        dense[b] = u_ref[0, where] * found

    inv = inv_ref[0]
    diag_ref[0] = dot_t(inv, inv)

    def plane_part(plane, part):
        lane = jnp.where(part == 0, y, 1 - y)
        return plane * plane_cols + lane * col_count

    for part in range(2):
        for i in range(col_count):
            moved[z, part * col_count + i] = dense[plane_part(z, part) + i]

    pl.semaphore_wait(barrier, planes - 1 + 1 + rows - 1)

    def y_copy(c):
        rng = pl.ds(c * step_rows, step_rows)
        return pltpu.make_async_remote_copy(
            sigma_ref.at[rng], other.at[rng], y_send.at[c], y_recv.at[c], at(z, 1 - y), MESH
        )

    def w_copy(target):
        return pltpu.make_async_remote_copy(
            dense.at[pl.ds(plane_part(target, half), col_count)],
            moved.at[z, pl.ds(half * col_count, col_count)],
            w_send.at[target],
            w_recv.at[z],
            at(target),
            MESH,
        )

    def w_arrival(source):
        mine = moved.at[source, pl.ds(half * col_count, col_count)]
        return pltpu.make_async_remote_copy(
            mine, mine, w_send.at[source], w_recv.at[source], at(source), MESH
        )

    def f_copy(source):
        mine = moved.at[source, pl.ds(half * col_count, col_count)]
        return pltpu.make_async_remote_copy(
            mine, mine, f_send.at[source], f_recv.at[source], at(z, None, mate), MESH
        )

    def f_arrival(source):
        theirs = moved.at[source, pl.ds((1 - half) * col_count, col_count)]
        return pltpu.make_async_remote_copy(
            theirs, theirs, f_send.at[source], f_recv.at[source], at(z, None, mate), MESH
        )

    def r_copy(d, c, h, slot, target):
        rng, lines = pl.ds(c * step_rows, step_rows), pl.ds(h * (width // 2), width // 2)
        return pltpu.make_async_remote_copy(
            sums.at[d, rng, lines],
            came.at[slot, rng, lines],
            r_send.at[d, 2 * c + h],
            r_recv.at[slot, 2 * c + h],
            at(target),
            MESH,
        )

    def r_arrival(slot, c, h):
        rng, lines = pl.ds(c * step_rows, step_rows), pl.ds(h * (width // 2), width // 2)
        return pltpu.make_async_remote_copy(
            came.at[slot, rng, lines],
            came.at[slot, rng, lines],
            r_send.at[0, 2 * c + h],
            r_recv.at[slot, 2 * c + h],
            at(z, 1 - y),
            MESH,
        )

    for c in range(chunks):
        y_copy(c).start()

    @pl.loop(0, planes - 1)
    def _(n):
        w_copy(order(n)).start()

    def forward(source):
        w_arrival(source).wait_recv()
        f_copy(source).start()

    def load_w(d):
        for i in range(plane_cols):
            high, low = split(moved[d, i])
            w_cat[i * width : (i + 1) * width, :width] = high
            w_cat[i * width : (i + 1) * width, width:] = low

    def convert(c):
        for q in range(step_rows):
            a = c * step_rows + q
            for source, base in ((sigma_ref, 0), (other, col_count)):
                for i in range(col_count):
                    high, low = split(source[a, i])
                    lanes = slice((base + i) * width, (base + i + 1) * width)
                    sig_hi[a, :, lanes] = high
                    sig_lo[a, :, lanes] = low

    def product(a):
        both = jnp.dot(sig_hi[a], w_cat[...], preferred_element_type=jnp.float32)
        low = jnp.dot(sig_lo[a], w_cat[:, :width], preferred_element_type=jnp.float32)
        return both[:, :width] + (both[:, width:] + low)

    forward(order(0))

    @pl.loop(0, planes - 1)
    def _(n):
        d = order(n)
        right = d > z
        f_arrival(d).wait_recv()
        load_w(d)
        has_up = jnp.where(right, z > 0, z < planes - 1)
        target = jnp.where(right, z + 1, z - 1)
        slot = jnp.where(right, d, jnp.where(d == z - 1, planes, d))
        for c in range(chunks):

            @pl.when(n == 0)
            def _():
                y_copy(c).wait_recv()
                convert(c)

            for q in range(step_rows):
                a = c * step_rows + q
                sums[d, a] = product(a)

            for h in range(2):
                lines = slice(h * (width // 2), (h + 1) * (width // 2))

                @pl.when(has_up)
                def _():
                    r_arrival(d, c, h).wait_recv()
                    for q in range(step_rows):
                        a = c * step_rows + q
                        sums[d, a, lines] += came[d, a, lines]

                r_copy(d, c, h, slot, target).start()

            if c == 0:

                @pl.when(n + 1 < planes - 1)
                def _():
                    forward(order(n + 1))

    load_w(z)
    for a in range(row_count):
        sums[z, a] = product(a)
    row_start = row * row_count
    total = jnp.zeros((width, width), jnp.float32)
    for c in range(chunks):

        @pl.when(z > 0)
        def _():
            r_arrival(z, c, 0).wait_recv()
            r_arrival(z, c, 1).wait_recv()
            for q in range(step_rows):
                a = c * step_rows + q
                sums[z, a] += came[z, a]

        @pl.when(z < planes - 1)
        def _():
            r_arrival(planes, c, 0).wait_recv()
            r_arrival(planes, c, 1).wait_recv()
            for q in range(step_rows):
                a = c * step_rows + q
                sums[z, a] += came[planes, a]

        for q in range(step_rows):
            a = c * step_rows + q
            found, _ = member(row_start + a)
            panel = -sums[z, a] * found
            panel_ref[0, a] = panel
            total += dot_t(dense[row_start + a], panel)
    share[...] = total

    def d_copy(o):
        return pltpu.make_async_remote_copy(
            share,
            shares.at[o - 1],
            d_send.at[o - 1],
            d_recv.at[o - 1],
            at(z, None, lax.rem(row + o, rows)),
            MESH,
        )

    for o in range(1, rows):
        d_copy(o).start()
    diag_ref[0] -= total
    for o in range(1, rows):
        d_copy(o).wait_recv()
        diag_ref[0] -= shares[o - 1]

    for o in range(1, rows):
        d_copy(o).wait_send()
    for c in range(chunks):
        y_copy(c).wait_send()

    @pl.loop(0, planes - 1)
    def _(n):
        d = order(n)
        w_copy(d).wait_send()
        f_copy(d).wait_send()
        for c in range(chunks):
            for h in range(2):
                r_copy(d, c, h, d, d).wait_send()


def local(sigma_anc, panel_u, structure, diag_inv):
    row_count, col_count, width = sigma_anc.shape[0], sigma_anc.shape[1], sigma_anc.shape[2]
    cols, rows = lax.axis_size("col"), lax.axis_size("row")
    planes = cols // 2
    plane_cols = 2 * col_count
    chunks = next(c for c in (4, 2, 1) if row_count % c == 0)
    block = (width, width)
    f32, bf16 = jnp.float32, jnp.bfloat16
    vmem = pl.BlockSpec(memory_space=pltpu.VMEM)
    dma = pltpu.SemaphoreType.DMA
    return pl.pallas_call(
        functools.partial(kernel, planes, rows, chunks),
        out_shape=(
            jax.ShapeDtypeStruct((1, row_count, *block), f32),
            jax.ShapeDtypeStruct((1, *block), f32),
        ),
        in_specs=[vmem, vmem, pl.BlockSpec(memory_space=pltpu.SMEM), vmem],
        out_specs=(vmem, vmem),
        scratch_shapes=[
            pltpu.VMEM((cols * col_count, *block), f32),
            pltpu.VMEM((planes, plane_cols, *block), f32),
            pltpu.VMEM((row_count, col_count, *block), f32),
            pltpu.VMEM((row_count, width, plane_cols * width), bf16),
            pltpu.VMEM((row_count, width, plane_cols * width), bf16),
            pltpu.VMEM((plane_cols * width, 2 * width), bf16),
            pltpu.VMEM((planes, row_count, *block), f32),
            pltpu.VMEM((planes + 1, row_count, *block), f32),
            pltpu.VMEM(block, f32),
            pltpu.VMEM((rows - 1, *block), f32),
            dma((chunks,)),
            dma((chunks,)),
            dma((planes,)),
            dma((planes,)),
            dma((planes,)),
            dma((planes,)),
            dma((planes, 2 * chunks)),
            dma((planes + 1, 2 * chunks)),
            dma((rows - 1,)),
            dma((rows - 1,)),
        ],
        compiler_params=pltpu.CompilerParams(
            collective_id=0, has_side_effects=True, vmem_limit_bytes=60 * 1024 * 1024
        ),
    )(sigma_anc, panel_u, structure, diag_inv)


def solution(mesh):
    placed = (
        P("row", "col", None, None),
        P("col", None, None, None),
        P("col", None),
        P("col", None, None),
    )
    return jax.shard_map(
        local,
        mesh=mesh,
        in_specs=placed,
        out_specs=(P("col", "row", None, None), P("col", None, None)),
        check_vma=False,
    )
```
